32 devices in a mesh: gx: 16 (over z, y, x), gy: 2 (over core).
Axes of the slice: x: 2, y: 2, z: 4, core: 2. Of those that a mesh axis runs over, the one named last changes fastest.
Arguments:
- features: bfloat16 [16, 2, 8, 128, 256], P('gx', 'gy'), may hold values from -6 to 6
- kernel_weight: bfloat16 [27, 256, 256], P(None, 'gy'), may hold values from -0.109375 to 0.109375
- channel_bias: float32 [256], replicated, may hold values from -3 to 3
- send_list: int32 [16, 2, 2], P('gx', 'gy'), may hold values from 0 to 7
- rule_source: int32 [16, 2, 27, 4], P('gx', 'gy'), may hold values from 0 to 23
- rule_target: int32 [16, 2, 27, 4], P('gx', 'gy'), may hold values from 0 to 7
- live_counts: int32 [16, 2, 27], P('gx', 'gy'), may hold values from 1 to 4, as said below
- out_grad: bfloat16 [16, 2, 8, 128, 256], P('gx', 'gy'), may hold values from -6 to 6
Outputs:
- outputs: bfloat16 [16, 2, 8, 128, 256], P('gx', 'gy')
- feat_grad: bfloat16 [16, 2, 8, 128, 256], P('gx', 'gy')
- weight_grad: float32 [27, 256, 256], P(None, 'gy')
The draws below stay inside these ranges and needn't reach their ends.
Inputs may be any that keep to these rules, and one draw needn't show every extreme that they name: `rule_source`: index into the device's block table of its 8 own blocks followed by 2 blocks from each of the eight directions. `rule_target`: an own block of the device. `send_list`: an own block of the device; a block may appear more than once. `live_counts`: slots from this count up to 3 are padding whose indices carry no meaning.
All inputs are finite; a program needn't handle non-finite values.
Results may differ from the reference program's by a relative error of at most 0.007.
Values may be sent and summed in bfloat16 or wider, within the bound.
A program may use at most 128 MiB of HBM per device.

```python
import jax
import jax.numpy as jnp
from jax import lax

C = 256
KVOL = 27
ROWS = 128
BLK = 8
HB = 2
P_SIZE = 4
N_GX = 16
N_GY = 2


def draw_live_counts(key, part):
    first_key, second_key, third_key = jax.random.split(key, 3)
    density = jax.random.randint(first_key, (N_GX, N_GY, 1), 1, 3)
    base_count = jax.random.randint(second_key, (N_GX, N_GY, KVOL), 1, 3)
    counts = jnp.minimum(density * base_count, P_SIZE).reshape(-1)
    position = jax.random.randint(third_key, (), 0, N_GX * N_GY * KVOL)
    counts = counts.at[position].set(P_SIZE)
    return counts.reshape(N_GX, N_GY, KVOL).astype(jnp.int32)


def place_ends(result, stream_key, smallest, high):
    dims = result.shape
    spot = [jax.random.randint(jax.random.fold_in(stream_key, axis), (), 0, dims[axis]) for axis in range(len(dims))]
    result = result.at[tuple(spot)].set(smallest)
    longest = dims.index(max(dims))
    spot[longest] = (spot[longest] + 1) % dims[longest]
    return result.at[tuple(spot)].set(high)


def block_scale(stream_key, dims, shards, low, high):
    loudness = 1.0
    for axis_at, blocks in shards:
        draws = jax.random.uniform(jax.random.fold_in(jax.random.fold_in(stream_key, 6), axis_at), (blocks,), jnp.float32, low / len(shards), high / len(shards))
        loudness = loudness * jnp.repeat(jnp.exp(draws), dims[axis_at] // blocks).reshape((-1,) + (1,) * (len(dims) - 1 - axis_at))
    return loudness


def centred(stream_key, shape, scale, reach, shards=(), kind=jnp.bfloat16):
    loudness = block_scale(stream_key, shape, shards, -0.22, 0.18) if shards else 1.0
    result = jax.random.normal(stream_key, shape, jnp.float32) * scale * loudness
    return jnp.minimum(jnp.maximum(result, -reach), reach).astype(kind)


def setup_inputs(seed: int = 0) -> dict:
    keys = jax.random.split(jax.random.key(seed), 9)
    return {
        "features": centred(keys[0], (N_GX, N_GY, BLK, ROWS, C), 1.0, 6.0, ((0, 16), (1, 2))),
        "kernel_weight": centred(keys[1], (KVOL, C, C), (C * KVOL * P_SIZE // BLK) ** -0.5, 0.109375, ((1, 2),)),
        "channel_bias": centred(keys[2], (C,), 0.5, 3.0, (), jnp.float32),
        "send_list": place_ends(jax.random.randint(keys[3], (N_GX, N_GY, HB), 0, BLK), jax.random.fold_in(keys[3], 1), 0, BLK - 1).astype(jnp.int32),
        "rule_source": place_ends(jax.random.randint(keys[4], (N_GX, N_GY, KVOL, P_SIZE), 0, BLK + 8 * HB), jax.random.fold_in(keys[4], 1), 0, (BLK + 8 * HB) - 1).astype(jnp.int32),
        "rule_target": place_ends(jax.random.randint(keys[5], (N_GX, N_GY, KVOL, P_SIZE), 0, BLK), jax.random.fold_in(keys[5], 1), 0, BLK - 1).astype(jnp.int32),
        "live_counts": draw_live_counts(jax.random.fold_in(keys[8], 71), 0),
        "out_grad": centred(keys[7], (N_GX, N_GY, BLK, ROWS, C), 1.0, 6.0, ((0, 16), (1, 2))),
    }


def device_pass(feats, neighbour, kernel_weight, channel_bias, rule_source, rule_target, live_counts, out_grad):
    blocks = feats.shape[0]
    rows_per = feats.shape[1]
    width = feats.shape[2]
    block_table = jnp.concatenate([feats, neighbour.reshape((-1, rows_per, width))], axis=0)
    total_blocks = block_table.shape[0]
    kvol, slots = rule_source.shape
    slot_index = jnp.arange(slots, dtype=jnp.int32)
    live_two = slot_index[None, :] < live_counts[:, None]
    live_mask = live_two.reshape(-1)
    sources = rule_source.reshape(-1)
    targets = rule_target.reshape(-1)
    gathered = block_table[sources].reshape(kvol, slots, rows_per, width)
    products = jnp.einsum("kprc,kcd->kprd", gathered.astype(jnp.float32), kernel_weight.astype(jnp.float32))
    products = products.reshape(kvol * slots, rows_per, width)
    scatter_out = ((targets[None, :] == jnp.arange(blocks, dtype=jnp.int32)[:, None]) & live_mask[None, :]).astype(jnp.float32)
    preact = jnp.einsum("bq,qrd->brd", scatter_out, products, precision=lax.Precision.HIGHEST) + channel_bias
    outputs = jax.nn.silu(preact).astype(jnp.bfloat16)
    sigmoid_vals = jax.nn.sigmoid(preact)
    dpre = (out_grad.astype(jnp.float32) * sigmoid_vals * (1.0 + preact * (1.0 - sigmoid_vals))).astype(jnp.bfloat16)
    picked = dpre[targets].reshape(kvol, slots, rows_per, width)
    picked_live = jnp.where(live_two[:, :, None, None], picked, jnp.zeros_like(picked))
    backs = jnp.einsum("kprd,kcd->kprc", picked.astype(jnp.float32), kernel_weight.astype(jnp.float32))
    backs = backs.reshape(kvol * slots, rows_per, width)
    scatter_in = ((sources[None, :] == jnp.arange(total_blocks, dtype=jnp.int32)[:, None]) & live_mask[None, :]).astype(jnp.float32)
    table_grad = jnp.einsum("tq,qrc->trc", scatter_in, backs, precision=lax.Precision.HIGHEST)
    wpart = jnp.einsum("kprc,kprd->kcd", gathered.astype(jnp.float32), picked_live.astype(jnp.float32))
    wpart = lax.optimization_barrier(wpart.astype(jnp.bfloat16)).astype(jnp.float32)
    return outputs, table_grad[:blocks], table_grad[blocks:].reshape((8, -1, rows_per, width)), wpart


def reference(features, kernel_weight, channel_bias, send_list, rule_source, rule_target, live_counts, out_grad):
    grid_x = features.shape[0]
    grid_y = features.shape[1]
    boundary = jax.vmap(jax.vmap(lambda block_feats, chosen: block_feats[chosen]))(features, send_list)
    padded = jnp.pad(boundary, ((1, 1), (1, 1), (0, 0), (0, 0), (0, 0)))
    directions = [(shift_x, shift_y) for shift_x in (-1, 0, 1) for shift_y in (-1, 0, 1) if not (shift_x == 0 and shift_y == 0)]
    neighbour = jnp.stack([padded[1 + shift_x:1 + shift_x + grid_x, 1 + shift_y:1 + shift_y + grid_y] for shift_x, shift_y in directions], axis=2)
    devices = grid_x * grid_y

    def flatten(array):
        return array.reshape((devices,) + array.shape[2:])

    def one_device(carry, items):
        outs, own, halo_part, wpart = device_pass(items[0], items[1], kernel_weight, channel_bias, items[2], items[3], items[4], items[5])
        return carry + wpart, (outs, own, halo_part)

    start_grad = jnp.zeros(kernel_weight.shape, jnp.float32)
    weight_sum, (outputs, own_grad, halo_grad) = lax.scan(one_device, start_grad, (flatten(features), flatten(neighbour), flatten(rule_source), flatten(rule_target), flatten(live_counts), flatten(out_grad)))
    halo_grad = halo_grad.reshape((grid_x, grid_y) + halo_grad.shape[1:])
    returned = jnp.zeros(boundary.shape, jnp.float32)
    for direction_index, (shift_x, shift_y) in enumerate(directions):
        padded_grad = jnp.pad(halo_grad[:, :, direction_index], ((1, 1), (1, 1), (0, 0), (0, 0), (0, 0)))
        returned = returned + padded_grad[1 - shift_x:1 - shift_x + grid_x, 1 - shift_y:1 - shift_y + grid_y]
    blocks = features.shape[2]
    placement = (send_list[:, :, None, :] == jnp.arange(blocks, dtype=jnp.int32)[:, None]).astype(jnp.float32)
    feat_grad = own_grad.reshape(features.shape) + jnp.einsum("xybh,xyhrc->xybrc", placement, returned, precision=lax.Precision.HIGHEST)
    weight_grad = weight_sum * (1.0 / features.shape[3])
    return outputs.reshape(features.shape), feat_grad.astype(jnp.bfloat16), weight_grad
```

```python
import functools

import jax
import jax.numpy as jnp
from jax import lax
from jax.experimental import pallas as pl
from jax.experimental.pallas import tpu as pltpu
from jax.sharding import PartitionSpec as P

MESH = pl.DeviceIdType.MESH
VMEM = pltpu.VMEM
SMEM = pltpu.SMEM
DIRECTIONS = [(sx, sy) for sx in (-1, 0, 1) for sy in (-1, 0, 1) if (sx, sy) != (0, 0)]
LANES = 128
TILE = 16
GROUPS = 9
ROTATIONS = 3


def inside(i, j, nx, ny):
    return (i >= 0) & (i < nx) & (j >= 0) & (j < ny)


def clipped(i, j, nx, ny):
    return jnp.clip(i, 0, nx - 1), jnp.clip(j, 0, ny - 1)


def greet_neighbours(barrier, me_x, me_y, nx, ny):
    total = 0
    for sx, sy in DIRECTIONS:
        there = inside(me_x + sx, me_y + sy, nx, ny)

        @pl.when(there)
        def _():
            pl.semaphore_signal(
                barrier, inc=1, device_id=(me_x + sx, me_y + sy), device_id_type=MESH
            )

        total = total + there.astype(jnp.int32)
    return total


def greet_column(barrier, me_x, me_y, ny):
    for step in range(1, ny):
        pl.semaphore_signal(
            barrier, inc=1, device_id=(me_x, lax.rem(me_y + step, ny)), device_id_type=MESH
        )
    return ny - 1


def exchange_kernel(
    nx, ny, send_ref, feats_ref, weight_ref, halo_ref, full_ref, shared, hsend, hrecv, wsend, wrecv
):
    me_x, me_y = lax.axis_index("gx"), lax.axis_index("gy")
    barrier = pltpu.get_barrier_semaphore()
    expected = greet_neighbours(barrier, me_x, me_y, nx, ny) + greet_column(
        barrier, me_x, me_y, ny
    )
    for s in range(shared.shape[0]):
        shared[s] = feats_ref[send_ref[s]]
    pl.semaphore_wait(barrier, expected)

    def halo_copy(d, i, j):
        return pltpu.make_async_remote_copy(
            src_ref=shared,
            dst_ref=halo_ref.at[d],
            send_sem=hsend.at[d],
            recv_sem=hrecv.at[d],
            device_id=(i, j),
            device_id_type=MESH,
        )

    def weight_copy(step, owner):
        return pltpu.make_async_remote_copy(
            src_ref=weight_ref,
            dst_ref=full_ref.at[:, owner],
            send_sem=wsend.at[step],
            recv_sem=wrecv.at[step],
            device_id=(me_x, lax.rem(me_y + step, ny)),
            device_id_type=MESH,
        )

    for d, (sx, sy) in enumerate(DIRECTIONS):

        @pl.when(inside(me_x - sx, me_y - sy, nx, ny))
        def _():
            halo_copy(d, me_x - sx, me_y - sy).start()

    for step in range(1, ny):
        weight_copy(step, me_y).start()
    full_ref[:, me_y] = weight_ref[...]
    for d, (sx, sy) in enumerate(DIRECTIONS):
        there = inside(me_x + sx, me_y + sy, nx, ny)

        @pl.when(jnp.logical_not(there))
        def _():
            halo_ref[d] = jnp.zeros(halo_ref.shape[1:], halo_ref.dtype)

        @pl.when(there)
        def _():
            halo_copy(d, me_x + sx, me_y + sy).wait_recv()

        @pl.when(inside(me_x - sx, me_y - sy, nx, ny))
        def _():
            halo_copy(d, me_x - sx, me_y - sy).wait_send()

    for step in range(1, ny):
        weight_copy(step, lax.rem(me_y - step + ny, ny)).wait_recv()
        weight_copy(step, me_y).wait_send()


def compute_kernel(
    slots,
    source_ref,
    target_ref,
    count_ref,
    feats_ref,
    halo_ref,
    weight_ref,
    bias_ref,
    cot_ref,
    out_ref,
    own_ref,
    borrowed_ref,
    wpart_ref,
    table,
    pre,
    dpre,
    grad,
):
    blocks, rows, width = feats_ref.shape
    kvol = weight_ref.shape[0]
    ny, tiles = wpart_ref.shape[:2]
    share = width // ny
    share_tiles = share // TILE
    for b in range(blocks):
        table[b] = feats_ref[b]
        pre[b] = jnp.broadcast_to(bias_ref[...], (rows, width))
    for t in range(halo_ref.shape[0]):
        table[blocks + t] = halo_ref[t]
    for t in range(grad.shape[0]):
        grad[t] = jnp.zeros((rows, width), jnp.float32)

    def by_count(k, work):
        live = count_ref[k]
        for amount in range(1, slots + 1):

            @pl.when(live == amount)
            def _():
                work(
                    [source_ref[k * slots + q] for q in range(amount)],
                    [target_ref[k * slots + q] for q in range(amount)],
                )

    def forward(k, carry):
        def work(sources, targets):
            taken = jnp.concatenate([table[s] for s in sources], axis=0)
            made = jnp.dot(taken, weight_ref[k], preferred_element_type=jnp.float32)
            for q, target in enumerate(targets):
                pre[target] += made[q * rows : (q + 1) * rows]

        by_count(k, work)
        return carry

    lax.fori_loop(0, kvol, forward, 0)

    def activate(b, carry):
        value = pre[b]
        sig = jax.nn.sigmoid(value)
        out_ref[b] = (value * sig).astype(out_ref.dtype)
        dpre[b] = (cot_ref[b].astype(jnp.float32) * sig * (1.0 + value * (1.0 - sig))).astype(
            dpre.dtype
        )
        return carry

    lax.fori_loop(0, blocks, activate, 0)

    filled = 2 * kvol * share_tiles
    if filled < tiles:
        for y in range(ny):
            wpart_ref[y, filled:] = jnp.zeros((tiles - filled, TILE, LANES), wpart_ref.dtype)

    def backward(k, carry):
        def work(sources, targets):
            taken = jnp.concatenate([table[s] for s in sources], axis=0)
            pulled = jnp.concatenate([dpre[t] for t in targets], axis=0)
            back = lax.dot_general(
                pulled, weight_ref[k], (((1,), (1,)), ((), ())), preferred_element_type=jnp.float32
            )
            for q, source in enumerate(sources):
                grad[source] += back[q * rows : (q + 1) * rows]
            part = lax.dot_general(
                taken, pulled, (((0,), (0,)), ((), ())), preferred_element_type=jnp.float32
            ).astype(wpart_ref.dtype)
            for y in range(ny):
                for h in range(width // LANES):
                    piece = part[y * share : (y + 1) * share, h * LANES : (h + 1) * LANES]
                    wpart_ref[y, pl.ds((h * kvol + k) * share_tiles, share_tiles)] = piece.reshape(
                        share_tiles, TILE, LANES
                    )

        by_count(k, work)
        return carry

    lax.fori_loop(0, kvol, backward, 0)
    for b in range(blocks):
        own_ref[b] = grad[b]
    for t in range(borrowed_ref.shape[0]):
        borrowed_ref[t] = grad[blocks + t].astype(borrowed_ref.dtype)


def reduce_kernel(
    nx,
    ny,
    wpart_ref,
    borrowed_ref,
    sum_ref,
    returned_ref,
    work,
    yland,
    xland,
    hland,
    ysend,
    yrecv,
    rsend,
    rrecv,
    gsend,
    grecv,
    hsend,
    hrecv,
):
    me_x, me_y = lax.axis_index("gx"), lax.axis_index("gy")
    groups = work.shape[0]
    steps = nx.bit_length() - 1
    bits = [lax.rem(me_x // (1 << b), 2) for b in range(steps)]
    partners = [me_x + (1 - 2 * bits[b]) * (1 << b) for b in range(steps)]

    barrier = pltpu.get_barrier_semaphore()
    expected = greet_neighbours(barrier, me_x, me_y, nx, ny) + greet_column(
        barrier, me_x, me_y, ny
    )
    for b in range(steps):
        pl.semaphore_signal(barrier, inc=1, device_id=(partners[b], me_y), device_id_type=MESH)
    pl.semaphore_wait(barrier, expected + steps)

    def halo_copy(d, i, j):
        return pltpu.make_async_remote_copy(
            src_ref=borrowed_ref.at[d],
            dst_ref=hland.at[d],
            send_sem=hsend.at[d],
            recv_sem=hrecv.at[d],
            device_id=(i, j),
            device_id_type=MESH,
        )

    def column_copy(step, g):
        other = lax.rem(me_y + step, ny)
        return pltpu.make_async_remote_copy(
            src_ref=wpart_ref.at[other, g],
            dst_ref=yland.at[step - 1, g],
            send_sem=ysend.at[step - 1, g],
            recv_sem=yrecv.at[step - 1, g],
            device_id=(me_x, other),
            device_id_type=MESH,
        )

    orders = [[(s + g % ROTATIONS) % steps for s in range(steps)] for g in range(groups)]
    starts = []
    for g in range(groups):
        at = [0]
        for s in range(steps):
            at.append(at[-1] + bits[orders[g][s]] * (nx >> (s + 1)))
        starts.append(at)

    def scatter_copy(g, s):
        half = nx >> (s + 1)
        bit = bits[orders[g][s]]
        away = starts[g][s] + (1 - bit) * half
        return pltpu.make_async_remote_copy(
            src_ref=work.at[g, pl.ds(away, half)],
            dst_ref=xland.at[g, pl.ds(nx - 2 * half, half)],
            send_sem=rsend.at[s, g],
            recv_sem=rrecv.at[s, g],
            device_id=(partners[orders[g][s]], me_y),
            device_id_type=MESH,
        )

    def gather_copy(g, s, landing):
        half = nx >> (s + 1)
        bit = bits[orders[g][s]]
        mine = starts[g][s + 1]
        place = starts[g][s] + (1 - bit) * half if landing else mine
        return pltpu.make_async_remote_copy(
            src_ref=sum_ref.at[g, pl.ds(mine, half)],
            dst_ref=sum_ref.at[g, pl.ds(place, half)],
            send_sem=gsend.at[s, g],
            recv_sem=grecv.at[s, g],
            device_id=(partners[orders[g][s]], me_y),
            device_id_type=MESH,
        )

    for g in range(groups):
        for step in range(1, ny):
            column_copy(step, g).start()
    for d, (sx, sy) in enumerate(DIRECTIONS):

        @pl.when(inside(me_x + sx, me_y + sy, nx, ny))
        def _():
            halo_copy(d, me_x + sx, me_y + sy).start()

    for g in range(groups):
        value = wpart_ref[me_y, g].astype(jnp.float32)
        for step in range(1, ny):
            column_copy(step, g).wait_recv()
            value = value + yland[step - 1, g].astype(jnp.float32)
        work[g] = value.astype(work.dtype)
        scatter_copy(g, 0).start()

    for s in range(steps):
        half = nx >> (s + 1)
        for g in range(groups):
            scatter_copy(g, s).wait_recv()
            keep = pl.ds(starts[g][s + 1], half)
            value = work[g, keep].astype(jnp.float32) + xland[
                g, pl.ds(nx - 2 * half, half)
            ].astype(jnp.float32)
            if s < steps - 1:
                work[g, keep] = value.astype(work.dtype)
                scatter_copy(g, s + 1).start()
            else:
                sum_ref[g, keep] = value.astype(sum_ref.dtype)
                gather_copy(g, s, False).start()

    returned_ref[...] = jnp.zeros(returned_ref.shape, jnp.float32)
    for d, (sx, sy) in enumerate(DIRECTIONS):

        @pl.when(inside(me_x - sx, me_y - sy, nx, ny))
        def _():
            halo_copy(d, me_x - sx, me_y - sy).wait_recv()
            returned_ref[...] += hland[d].astype(jnp.float32)

    for s in reversed(range(steps)):
        for g in range(groups):
            gather_copy(g, s, True).wait_recv()
            if s > 0:
                gather_copy(g, s - 1, False).start()

    for g in range(groups):
        for step in range(1, ny):
            column_copy(step, g).wait_send()
        for s in range(steps):
            scatter_copy(g, s).wait_send()
            gather_copy(g, s, False).wait_send()
    for d, (sx, sy) in enumerate(DIRECTIONS):

        @pl.when(inside(me_x + sx, me_y + sy, nx, ny))
        def _():
            halo_copy(d, me_x + sx, me_y + sy).wait_send()


def on_device(
    nx,
    ny,
    features,
    kernel_weight,
    channel_bias,
    send_list,
    rule_source,
    rule_target,
    live_counts,
    out_grad,
):
    feats = features[0, 0]
    blocks, rows, width = feats.shape
    shared = send_list[0, 0]
    shared_count = shared.shape[0]
    kvol, slots = rule_source.shape[2:]
    share = kernel_weight.shape[1]
    bf16, f32 = jnp.bfloat16, jnp.float32
    shape = jax.ShapeDtypeStruct
    vmem = pl.BlockSpec(memory_space=VMEM)
    smem = pl.BlockSpec(memory_space=SMEM)
    directions = len(DIRECTIONS)
    dma = pltpu.SemaphoreType.DMA

    halo, full = pl.pallas_call(
        functools.partial(exchange_kernel, nx, ny),
        out_shape=(
            shape((directions, shared_count, rows, width), bf16),
            shape((kvol, ny, share, width), bf16),
        ),
        in_specs=[smem, vmem, vmem],
        out_specs=(vmem, vmem),
        scratch_shapes=[
            VMEM((shared_count, rows, width), bf16),
            dma((directions,)),
            dma((directions,)),
            dma((ny,)),
            dma((ny,)),
        ],
        compiler_params=pltpu.CompilerParams(collective_id=0, has_side_effects=True),
    )(shared, feats, kernel_weight)

    borrowed_count = directions * shared_count
    used = (width // LANES) * kvol * (share // TILE)
    unit = GROUPS * nx
    tiles = -(-used // unit) * unit
    depth = tiles // unit
    outputs, own, borrowed, wpart = pl.pallas_call(
        functools.partial(compute_kernel, slots),
        out_shape=(
            shape((blocks, rows, width), bf16),
            shape((blocks, rows, width), f32),
            shape((borrowed_count, rows, width), bf16),
            shape((ny, tiles, TILE, LANES), bf16),
        ),
        in_specs=[smem, smem, smem, vmem, vmem, vmem, vmem, vmem],
        out_specs=(vmem, vmem, vmem, vmem),
        scratch_shapes=[
            VMEM((blocks + borrowed_count, rows, width), bf16),
            VMEM((blocks, rows, width), f32),
            VMEM((blocks, rows, width), bf16),
            VMEM((blocks + borrowed_count, rows, width), f32),
        ],
    )(
        rule_source.reshape(-1),
        rule_target.reshape(-1),
        live_counts.reshape(-1),
        feats,
        halo.reshape(borrowed_count, rows, width),
        full.reshape(kvol, width, width),
        channel_bias.reshape(1, width),
        out_grad[0, 0],
    )

    steps = nx.bit_length() - 1
    block = (depth, TILE, LANES)
    total, returned = pl.pallas_call(
        functools.partial(reduce_kernel, nx, ny),
        out_shape=(
            shape((GROUPS, nx) + block, bf16),
            shape((shared_count, rows, width), f32),
        ),
        in_specs=[vmem, vmem],
        out_specs=(vmem, vmem),
        scratch_shapes=[
            VMEM((GROUPS, nx) + block, bf16),
            VMEM((max(ny - 1, 1), GROUPS, nx) + block, bf16),
            VMEM((GROUPS, nx) + block, bf16),
            VMEM((directions, shared_count, rows, width), bf16),
            dma((max(ny - 1, 1), GROUPS)),
            dma((max(ny - 1, 1), GROUPS)),
            dma((steps, GROUPS)),
            dma((steps, GROUPS)),
            dma((steps, GROUPS)),
            dma((steps, GROUPS)),
            dma((directions,)),
            dma((directions,)),
        ],
        compiler_params=pltpu.CompilerParams(collective_id=1, has_side_effects=True),
    )(
        wpart.reshape((ny, GROUPS, nx) + block),
        borrowed.reshape(directions, shared_count, rows, width),
    )

    weight_grad = (
        total.reshape(tiles, TILE, LANES)[:used]
        .reshape(width // LANES, kvol, share, LANES)
        .transpose(1, 2, 0, 3)
        .reshape(kvol, share, width)
        .astype(f32)
    ) * (1.0 / rows)
    feat_grad = own
    for s in range(shared_count):
        hit = shared[s] == jnp.arange(blocks, dtype=jnp.int32)
        feat_grad = feat_grad + jnp.where(hit[:, None, None], returned[s][None], 0.0)
    return (outputs[None, None], feat_grad.astype(bf16)[None, None], weight_grad)


def solution(mesh):
    return jax.shard_map(
        functools.partial(on_device, mesh.shape["gx"], mesh.shape["gy"]),
        mesh=mesh,
        in_specs=(
            P("gx", "gy", None, None, None),
            P(None, "gy", None),
            P(),
            P("gx", "gy", None),
            P("gx", "gy", None, None),
            P("gx", "gy", None, None),
            P("gx", "gy", None),
            P("gx", "gy", None, None, None),
        ),
        out_specs=(
            P("gx", "gy", None, None, None),
            P("gx", "gy", None, None, None),
            P(None, "gy", None),
        ),
        check_vma=False,
    )
```

```python
import functools

import jax
import jax.numpy as jnp
from jax import lax
from jax.experimental import pallas as pl
from jax.experimental.pallas import tpu as pltpu
from jax.sharding import PartitionSpec as P

MESH = pl.DeviceIdType.MESH
VMEM = pltpu.VMEM
SMEM = pltpu.SMEM
LANES = 128
TILE = 16
KINDS = (2, 0, 1, 3, 0, 1, 0, 1, 0)
UNROLL = 3
VMEM_BYTES = 28 * 1024 * 1024


def greet_neighbours(barrier, me_x, me_y, nx, ny):
    total = 0
    for sx, sy in ((-1, 0), (1, 0), (0, -1), (0, 1)):
        x, y = me_x + sx, me_y + sy
        there = (x >= 0) & (x < nx) & (y >= 0) & (y < ny)

        @pl.when(there)
        def _():
            pl.semaphore_signal(barrier, inc=1, device_id=(x, y), device_id_type=MESH)

        total = total + there.astype(jnp.int32)
    return total


def greet_column(barrier, me_x, me_y, ny):
    for step in range(1, ny):
        pl.semaphore_signal(
            barrier, inc=1, device_id=(me_x, lax.rem(me_y + step, ny)), device_id_type=MESH
        )
    return ny - 1


def exists(index, count):
    return (index >= 0) & (index < count)


def exchange_kernel(
    nx, ny, send_ref, feats_ref, weight_ref, halo_ref, full_ref, xsend, xrecv, hsend, hrecv, wsend, wrecv
):
    me_x, me_y = lax.axis_index("gx"), lax.axis_index("gy")
    barrier = pltpu.get_barrier_semaphore()
    expected = greet_neighbours(barrier, me_x, me_y, nx, ny) + greet_column(
        barrier, me_x, me_y, ny
    )
    for s in range(halo_ref.shape[1]):
        halo_ref[4, s] = feats_ref[send_ref[s]]
    pl.semaphore_wait(barrier, expected)

    def x_copy(a, device_x):
        return pltpu.make_async_remote_copy(
            src_ref=halo_ref.at[4],
            dst_ref=halo_ref.at[3 * a + 1],
            send_sem=xsend.at[a // 2],
            recv_sem=xrecv.at[a // 2],
            device_id=(device_x, me_y),
            device_id_type=MESH,
        )

    def y_copy(a, b, device_y):
        return pltpu.make_async_remote_copy(
            src_ref=halo_ref.at[3 * a + 1],
            dst_ref=halo_ref.at[3 * a + b],
            send_sem=hsend.at[a, b // 2],
            recv_sem=hrecv.at[a, b // 2],
            device_id=(me_x, device_y),
            device_id_type=MESH,
        )

    def weight_copy(step, owner):
        return pltpu.make_async_remote_copy(
            src_ref=weight_ref,
            dst_ref=full_ref.at[:, owner],
            send_sem=wsend.at[step],
            recv_sem=wrecv.at[step],
            device_id=(me_x, lax.rem(me_y + step, ny)),
            device_id_type=MESH,
        )

    def to_column(a, act):
        for b in (0, 2):
            target = me_y + 1 - b

            @pl.when(exists(target, ny))
            def _():
                act(y_copy(a, b, target))

    for a in (0, 2):
        target = me_x + 1 - a

        @pl.when(exists(target, nx))
        def _():
            x_copy(a, target).start()

    to_column(1, lambda copy: copy.start())
    for step in range(1, ny):
        weight_copy(step, me_y).start()
    full_ref[:, me_y] = weight_ref[...]
    blank = jnp.zeros(halo_ref.shape[1:], halo_ref.dtype)
    for a in (0, 2):
        here = exists(me_x + a - 1, nx)

        @pl.when(jnp.logical_not(here))
        def _():
            halo_ref[3 * a + 1] = blank

        @pl.when(here)
        def _():
            x_copy(a, me_x + a - 1).wait_recv()
            to_column(a, lambda copy: copy.start())

    for a in range(3):
        for b in (0, 2):
            there = exists(me_x + a - 1, nx) & exists(me_y + b - 1, ny)

            @pl.when(jnp.logical_not(there))
            def _():
                halo_ref[3 * a + b] = blank

            @pl.when(there)
            def _():
                y_copy(a, b, me_y + b - 1).wait_recv()

        @pl.when(exists(me_x + a - 1, nx))
        def _():
            to_column(a, lambda copy: copy.wait_send())

    for a in (0, 2):
        target = me_x + 1 - a

        @pl.when(exists(target, nx))
        def _():
            x_copy(a, target).wait_send()

    for step in range(1, ny):
        weight_copy(step, lax.rem(me_y - step + ny, ny)).wait_recv()
        weight_copy(step, me_y).wait_send()


def compute_kernel(
    source_ref,
    target_ref,
    count_ref,
    feats_ref,
    halo_ref,
    weight_ref,
    bias_ref,
    cot_ref,
    out_ref,
    own_ref,
    borrowed_ref,
    wpart_ref,
    table,
    turned,
    pre,
    dpre,
    grad,
):
    blocks, rows, width = feats_ref.shape
    slots = source_ref.shape[0]
    kvol = weight_ref.shape[0]
    total_blocks = grad.shape[0] - 1
    shared_count = halo_ref.shape[1]
    ny, tiles = wpart_ref.shape[:2]
    share = width // ny
    share_tiles = share // TILE
    places = [(b, feats_ref.at[b]) for b in range(blocks)]
    at = blocks
    for d in range(9):
        if d != 4:
            for s in range(shared_count):
                places.append((at, halo_ref.at[d, s]))
                at += 1
    for t, ref in places:
        value = ref[...]
        table[t] = value
        turned[t] = value.T
    for b in range(blocks):
        pre[b] = jnp.broadcast_to(bias_ref[...], (rows, width))
    for t in range(total_blocks):
        grad[t] = jnp.zeros((rows, width), jnp.float32)
    pre[blocks] = jnp.zeros((rows, width), jnp.float32)
    grad[total_blocks] = jnp.zeros((rows, width), jnp.float32)
    dpre[blocks] = jnp.zeros((rows, width), dpre.dtype)

    def rules(k):
        live = count_ref[k]
        sources = [source_ref[q, k] for q in range(slots)]
        targets = [target_ref[q, k] for q in range(slots)]
        reads = [jnp.where(q < live, v, 0) for q, v in enumerate(sources)]
        spread = [jnp.where(q < live, v, total_blocks) for q, v in enumerate(sources)]
        targets = [jnp.where(q < live, v, blocks) for q, v in enumerate(targets)]
        return reads, spread, targets

    def forward(k, carry):
        reads, _, targets = rules(k)
        taken = jnp.concatenate([table[s] for s in reads], axis=0)
        made = jnp.dot(taken, weight_ref[k], preferred_element_type=jnp.float32)
        for q, target in enumerate(targets):
            pre[target] += made[q * rows : (q + 1) * rows]
        return carry

    lax.fori_loop(0, kvol, forward, 0, unroll=UNROLL)

    def activate(b, carry):
        value = pre[b]
        sig = jax.nn.sigmoid(value)
        out_ref[b] = (value * sig).astype(out_ref.dtype)
        dpre[b] = (cot_ref[b].astype(jnp.float32) * sig * (1.0 + value * (1.0 - sig))).astype(
            dpre.dtype
        )
        return carry

    lax.fori_loop(0, blocks, activate, 0)

    filled = 2 * kvol * share_tiles
    if filled < tiles:
        for y in range(ny):
            wpart_ref[y, filled:] = jnp.zeros((tiles - filled, TILE, LANES), wpart_ref.dtype)

    def backward(k, carry):
        reads, spread, targets = rules(k)
        pulled = jnp.concatenate([dpre[t] for t in targets], axis=0)
        taken = jnp.concatenate([turned[s] for s in reads], axis=1)
        part = jnp.dot(taken, pulled, preferred_element_type=jnp.float32).astype(wpart_ref.dtype)
        for y in range(ny):
            for h in range(width // LANES):
                piece = part[y * share : (y + 1) * share, h * LANES : (h + 1) * LANES]
                wpart_ref[y, pl.ds((h * kvol + k) * share_tiles, share_tiles)] = piece.reshape(
                    share_tiles, TILE, LANES
                )
        back = lax.dot_general(
            pulled, weight_ref[k], (((1,), (1,)), ((), ())), preferred_element_type=jnp.float32
        )
        for q, source in enumerate(spread):
            grad[source] += back[q * rows : (q + 1) * rows]
        return carry

    lax.fori_loop(0, kvol, backward, 0, unroll=UNROLL)
    for b in range(blocks):
        own_ref[b] = grad[b]
    at = blocks
    for d in range(9):
        for s in range(shared_count):
            if d == 4:
                borrowed_ref[d, s] = jnp.zeros((rows, width), borrowed_ref.dtype)
            else:
                borrowed_ref[d, s] = grad[at].astype(borrowed_ref.dtype)
                at += 1


def reduce_kernel(
    nx,
    ny,
    wpart_ref,
    borrowed_ref,
    sum_ref,
    returned_ref,
    work,
    yland,
    xland,
    side_land,
    column,
    x_land,
    ysend,
    yrecv,
    rsend,
    rrecv,
    gsend,
    grecv,
    hsend,
    hrecv,
    bsend,
    brecv,
):
    me_x, me_y = lax.axis_index("gx"), lax.axis_index("gy")
    groups = work.shape[0]
    steps = nx.bit_length() - 1
    bits = [lax.rem(me_x // (1 << b), 2) for b in range(steps)]
    partners = [me_x + (1 - 2 * bits[b]) * (1 << b) for b in range(steps)]

    barrier = pltpu.get_barrier_semaphore()
    expected = greet_neighbours(barrier, me_x, me_y, nx, ny) + greet_column(
        barrier, me_x, me_y, ny
    )
    for b in range(steps):
        pl.semaphore_signal(barrier, inc=1, device_id=(partners[b], me_y), device_id_type=MESH)
    pl.semaphore_wait(barrier, expected + steps)

    def side_copy(a, b):
        return pltpu.make_async_remote_copy(
            src_ref=borrowed_ref.at[3 * a + b],
            dst_ref=side_land.at[a, b // 2],
            send_sem=hsend.at[a, b // 2],
            recv_sem=hrecv.at[a, b // 2],
            device_id=(me_x, me_y + b - 1),
            device_id_type=MESH,
        )

    def back_copy(a):
        return pltpu.make_async_remote_copy(
            src_ref=column.at[a // 2],
            dst_ref=x_land.at[a // 2],
            send_sem=bsend.at[a // 2],
            recv_sem=brecv.at[a // 2],
            device_id=(me_x + a - 1, me_y),
            device_id_type=MESH,
        )

    def sides(act, sign):
        for a in range(3):
            for b in (0, 2):

                @pl.when(exists(me_x + a - 1, nx) & exists(me_y + sign * (b - 1), ny))
                def _():
                    act(a, b)

    def column_copy(step, g):
        other = lax.rem(me_y + step, ny)
        return pltpu.make_async_remote_copy(
            src_ref=wpart_ref.at[other, g],
            dst_ref=yland.at[step - 1, g],
            send_sem=ysend.at[step - 1, g],
            recv_sem=yrecv.at[step - 1, g],
            device_id=(me_x, other),
            device_id_type=MESH,
        )

    late = list(range(2, steps))
    kinds = [[0, 1] + late, [1, 0] + late, late + [0, 1], late + [1, 0]]
    orders = [kinds[kind] for kind in KINDS]
    starts = []
    for g in range(groups):
        at = [0]
        for s in range(steps):
            at.append(at[-1] + bits[orders[g][s]] * (nx >> (s + 1)))
        starts.append(at)

    def scatter_copy(g, s):
        half = nx >> (s + 1)
        bit = bits[orders[g][s]]
        away = starts[g][s] + (1 - bit) * half
        return pltpu.make_async_remote_copy(
            src_ref=work.at[g, pl.ds(away, half)],
            dst_ref=xland.at[g, pl.ds(nx - 2 * half, half)],
            send_sem=rsend.at[s, g],
            recv_sem=rrecv.at[s, g],
            device_id=(partners[orders[g][s]], me_y),
            device_id_type=MESH,
        )

    def gather_copy(g, s, landing):
        half = nx >> (s + 1)
        bit = bits[orders[g][s]]
        mine = starts[g][s + 1]
        place = starts[g][s] + (1 - bit) * half if landing else mine
        return pltpu.make_async_remote_copy(
            src_ref=sum_ref.at[g, pl.ds(mine, half)],
            dst_ref=sum_ref.at[g, pl.ds(place, half)],
            send_sem=gsend.at[s, g],
            recv_sem=grecv.at[s, g],
            device_id=(partners[orders[g][s]], me_y),
            device_id_type=MESH,
        )

    for g in range(groups):
        for step in range(1, ny):
            column_copy(step, g).start()
    sides(lambda a, b: side_copy(a, b).start(), 1)

    for g in range(groups):
        value = wpart_ref[me_y, g].astype(jnp.float32)
        for step in range(1, ny):
            column_copy(step, g).wait_recv()
            value = value + yland[step - 1, g].astype(jnp.float32)
        work[g] = value.astype(work.dtype)
        scatter_copy(g, 0).start()

    returned_ref[...] = jnp.zeros(returned_ref.shape, jnp.float32)
    for b in (0, 2):

        @pl.when(exists(me_y + 1 - b, ny))
        def _():
            side_copy(1, b).wait_recv()
            returned_ref[...] += side_land[1, b // 2].astype(jnp.float32)

    for a in (0, 2):

        @pl.when(exists(me_x + a - 1, nx))
        def _():
            for b in (0, 2):
                missing = jnp.logical_not(exists(me_y + 1 - b, ny))

                @pl.when(missing)
                def _():
                    side_land[a, b // 2] = jnp.zeros(side_land.shape[2:], side_land.dtype)

                @pl.when(jnp.logical_not(missing))
                def _():
                    side_copy(a, b).wait_recv()

            column[a // 2] = (
                borrowed_ref[3 * a + 1].astype(jnp.float32)
                + side_land[a, 0].astype(jnp.float32)
                + side_land[a, 1].astype(jnp.float32)
            ).astype(column.dtype)
            back_copy(a).start()

    for s in range(steps):
        half = nx >> (s + 1)
        for g in range(groups):
            scatter_copy(g, s).wait_recv()
            keep = pl.ds(starts[g][s + 1], half)
            value = work[g, keep].astype(jnp.float32) + xland[
                g, pl.ds(nx - 2 * half, half)
            ].astype(jnp.float32)
            if s < steps - 1:
                work[g, keep] = value.astype(work.dtype)
                scatter_copy(g, s + 1).start()
            else:
                sum_ref[g, keep] = value.astype(sum_ref.dtype)
                gather_copy(g, s, False).start()

    for a in (0, 2):

        @pl.when(exists(me_x + 1 - a, nx))
        def _():
            back_copy(a).wait_recv()
            returned_ref[...] += x_land[a // 2].astype(jnp.float32)

    for s in reversed(range(steps)):
        for g in range(groups):
            gather_copy(g, s, True).wait_recv()
            if s > 0:
                gather_copy(g, s - 1, False).start()

    for g in range(groups):
        for step in range(1, ny):
            column_copy(step, g).wait_send()
        for s in range(steps):
            scatter_copy(g, s).wait_send()
            gather_copy(g, s, False).wait_send()
    sides(lambda a, b: side_copy(a, b).wait_send(), 1)
    for a in (0, 2):

        @pl.when(exists(me_x + a - 1, nx))
        def _():
            back_copy(a).wait_send()


def finish_kernel(blocks, send_ref, total_ref, own_ref, returned_ref, weight_ref, feat_ref):
    per, share, width = weight_ref.shape
    rows = own_ref.shape[1]
    for h in range(width // LANES):
        weight_ref[:, :, h * LANES : (h + 1) * LANES] = total_ref[h].reshape(
            per, share, LANES
        ).astype(jnp.float32) * (1.0 / rows)
    at = jnp.minimum(pl.program_id(0), blocks - 1)
    value = own_ref[0]
    for s in range(returned_ref.shape[0]):
        value = value + jnp.where(send_ref[s] == at, returned_ref[s], 0.0)
    feat_ref[0] = value.astype(feat_ref.dtype)


def on_device(
    nx,
    ny,
    features,
    kernel_weight,
    channel_bias,
    send_list,
    rule_source,
    rule_target,
    live_counts,
    out_grad,
):
    feats = features[0, 0]
    blocks, rows, width = feats.shape
    shared = send_list[0, 0]
    shared_count = shared.shape[0]
    kvol, slots = rule_source.shape[2:]
    share = kernel_weight.shape[1]
    bf16, f32 = jnp.bfloat16, jnp.float32
    shape = jax.ShapeDtypeStruct
    vmem = pl.BlockSpec(memory_space=VMEM)
    smem = pl.BlockSpec(memory_space=SMEM)
    dma = pltpu.SemaphoreType.DMA
    squares = 9

    halo, full = pl.pallas_call(
        functools.partial(exchange_kernel, nx, ny),
        out_shape=(
            shape((squares, shared_count, rows, width), bf16),
            shape((kvol, ny, share, width), bf16),
        ),
        in_specs=[smem, vmem, vmem],
        out_specs=(vmem, vmem),
        scratch_shapes=[dma((2,)), dma((2,)), dma((3, 2)), dma((3, 2)), dma((ny,)), dma((ny,))],
        compiler_params=pltpu.CompilerParams(
            collective_id=0, has_side_effects=True, vmem_limit_bytes=VMEM_BYTES
        ),
    )(shared, feats, kernel_weight)

    total_blocks = blocks + (squares - 1) * shared_count
    used = (width // LANES) * kvol * (share // TILE)
    groups = len(KINDS)
    unit = groups * nx
    tiles = -(-used // unit) * unit
    depth = tiles // unit
    outputs, own, borrowed, wpart = pl.pallas_call(
        compute_kernel,
        out_shape=(
            shape((blocks, rows, width), bf16),
            shape((blocks, rows, width), f32),
            shape((squares, shared_count, rows, width), bf16),
            shape((ny, tiles, TILE, LANES), bf16),
        ),
        in_specs=[smem, smem, smem, vmem, vmem, vmem, vmem, vmem],
        out_specs=(vmem, vmem, vmem, vmem),
        scratch_shapes=[
            VMEM((total_blocks, rows, width), bf16),
            VMEM((total_blocks, width, rows), bf16),
            VMEM((blocks + 1, rows, width), f32),
            VMEM((blocks + 1, rows, width), bf16),
            VMEM((total_blocks + 1, rows, width), f32),
        ],
        compiler_params=pltpu.CompilerParams(vmem_limit_bytes=VMEM_BYTES),
    )(
        rule_source[0, 0].T,
        rule_target[0, 0].T,
        live_counts.reshape(-1),
        feats,
        halo,
        full.reshape(kvol, width, width),
        channel_bias.reshape(1, width),
        out_grad[0, 0],
    )

    steps = nx.bit_length() - 1
    block = (depth, TILE, LANES)
    boundary = (shared_count, rows, width)
    total, returned = pl.pallas_call(
        functools.partial(reduce_kernel, nx, ny),
        out_shape=(
            shape((groups, nx) + block, bf16),
            shape(boundary, f32),
        ),
        in_specs=[vmem, vmem],
        out_specs=(vmem, vmem),
        scratch_shapes=[
            VMEM((groups, nx) + block, bf16),
            VMEM((max(ny - 1, 1), groups, nx) + block, bf16),
            VMEM((groups, nx) + block, bf16),
            VMEM((3, 2) + boundary, bf16),
            VMEM((2,) + boundary, bf16),
            VMEM((2,) + boundary, bf16),
            dma((max(ny - 1, 1), groups)),
            dma((max(ny - 1, 1), groups)),
            dma((steps, groups)),
            dma((steps, groups)),
            dma((steps, groups)),
            dma((steps, groups)),
            dma((3, 2)),
            dma((3, 2)),
            dma((2,)),
            dma((2,)),
        ],
        compiler_params=pltpu.CompilerParams(
            collective_id=1, has_side_effects=True, vmem_limit_bytes=VMEM_BYTES
        ),
    )(wpart.reshape((ny, groups, nx) + block), borrowed)

    per = max(p for p in range(1, kvol + 1) if kvol % p == 0 and kvol // p >= blocks)
    halves, share_tiles = width // LANES, share // TILE

    def own_block(i):
        return (jnp.minimum(i, blocks - 1), 0, 0)

    weight_grad, feat_grad = pl.pallas_call(
        functools.partial(finish_kernel, blocks),
        grid=(kvol // per,),
        out_shape=(shape((kvol, share, width), f32), shape((blocks, rows, width), bf16)),
        in_specs=[
            smem,
            pl.BlockSpec((halves, per, share_tiles, TILE, LANES), lambda i: (0, i, 0, 0, 0)),
            pl.BlockSpec((1, rows, width), own_block),
            pl.BlockSpec(boundary, lambda i: (0, 0, 0)),
        ],
        out_specs=(
            pl.BlockSpec((per, share, width), lambda i: (i, 0, 0)),
            pl.BlockSpec((1, rows, width), own_block),
        ),
        compiler_params=pltpu.CompilerParams(vmem_limit_bytes=VMEM_BYTES),
    )(
        shared,
        total.reshape(tiles, TILE, LANES)[:used].reshape(halves, kvol, share_tiles, TILE, LANES),
        own,
        returned,
    )
    return (outputs[None, None], feat_grad[None, None], weight_grad)


def solution(mesh):
    return jax.shard_map(
        functools.partial(on_device, mesh.shape["gx"], mesh.shape["gy"]),
        mesh=mesh,
        in_specs=(
            P("gx", "gy", None, None, None),
            P(None, "gy", None),
            P(),
            P("gx", "gy", None),
            P("gx", "gy", None, None),
            P("gx", "gy", None, None),
            P("gx", "gy", None),
            P("gx", "gy", None, None, None),
        ),
        out_specs=(
            P("gx", "gy", None, None, None),
            P("gx", "gy", None, None, None),
            P(None, "gy", None),
        ),
        check_vma=False,
    )
```

```python
import functools

import jax
import jax.numpy as jnp
from jax import lax
from jax.experimental import pallas as pl
from jax.experimental.pallas import tpu as pltpu
from jax.sharding import PartitionSpec as P

MESH = pl.DeviceIdType.MESH
VMEM = pltpu.VMEM
SMEM = pltpu.SMEM
LANES = 128
TILE = 16
KINDS = (2, 0, 1, 3, 0, 1, 0, 1, 0)
WAVES = (0,) * 9
STAGGER = 1
HALO_AT = 4
UNROLL = 9
VMEM_BYTES = 28 * 1024 * 1024
EXCHANGE_BYTES = 28 * 1024 * 1024


def greet_neighbours(barrier, me_x, me_y, nx, ny):
    total = 0
    for sx, sy in ((-1, 0), (1, 0), (0, -1), (0, 1)):
        x, y = me_x + sx, me_y + sy
        there = (x >= 0) & (x < nx) & (y >= 0) & (y < ny)

        @pl.when(there)
        def _():
            pl.semaphore_signal(barrier, inc=1, device_id=(x, y), device_id_type=MESH)

        total = total + there.astype(jnp.int32)
    return total


def greet_column(barrier, me_x, me_y, ny):
    for step in range(1, ny):
        pl.semaphore_signal(
            barrier, inc=1, device_id=(me_x, lax.rem(me_y + step, ny)), device_id_type=MESH
        )
    return ny - 1


def exists(index, count):
    return (index >= 0) & (index < count)


def exchange_kernel(
    nx, ny, send_ref, feats_ref, weight_ref, halo_ref, full_ref, feats, lsem, xsend, xrecv, hsend, hrecv, wsend, wrecv
):
    me_x, me_y = lax.axis_index("gx"), lax.axis_index("gy")
    barrier = pltpu.get_barrier_semaphore()
    expected = greet_neighbours(barrier, me_x, me_y, nx, ny) + greet_column(
        barrier, me_x, me_y, ny
    )
    load = pltpu.make_async_copy(feats_ref, feats, lsem.at[0])
    load.start()
    keep = pltpu.make_async_copy(weight_ref, full_ref.at[:, me_y], lsem.at[1])
    keep.start()
    load.wait()
    for s in range(halo_ref.shape[1]):
        halo_ref[4, s] = feats[send_ref[s]]
    pl.semaphore_wait(barrier, expected)

    def x_copy(a, device_x):
        return pltpu.make_async_remote_copy(
            src_ref=halo_ref.at[4],
            dst_ref=halo_ref.at[3 * a + 1],
            send_sem=xsend.at[a // 2],
            recv_sem=xrecv.at[a // 2],
            device_id=(device_x, me_y),
            device_id_type=MESH,
        )

    def y_copy(a, b, device_y):
        return pltpu.make_async_remote_copy(
            src_ref=halo_ref.at[3 * a + 1],
            dst_ref=halo_ref.at[3 * a + b],
            send_sem=hsend.at[a, b // 2],
            recv_sem=hrecv.at[a, b // 2],
            device_id=(me_x, device_y),
            device_id_type=MESH,
        )

    def weight_copy(step, owner):
        return pltpu.make_async_remote_copy(
            src_ref=weight_ref,
            dst_ref=full_ref.at[:, owner],
            send_sem=wsend.at[step],
            recv_sem=wrecv.at[step],
            device_id=(me_x, lax.rem(me_y + step, ny)),
            device_id_type=MESH,
        )

    def to_column(a, act):
        for b in (0, 2):
            target = me_y + 1 - b

            @pl.when(exists(target, ny))
            def _():
                act(y_copy(a, b, target))

    for a in (0, 2):
        target = me_x + 1 - a

        @pl.when(exists(target, nx))
        def _():
            x_copy(a, target).start()

    to_column(1, lambda copy: copy.start())
    for step in range(1, ny):
        weight_copy(step, me_y).start()
    blank = jnp.zeros(halo_ref.shape[1:], halo_ref.dtype)
    for a in (0, 2):
        here = exists(me_x + a - 1, nx)

        @pl.when(jnp.logical_not(here))
        def _():
            halo_ref[3 * a + 1] = blank

        @pl.when(here)
        def _():
            x_copy(a, me_x + a - 1).wait_recv()
            to_column(a, lambda copy: copy.start())

    for a in range(3):
        for b in (0, 2):
            there = exists(me_x + a - 1, nx) & exists(me_y + b - 1, ny)

            @pl.when(jnp.logical_not(there))
            def _():
                halo_ref[3 * a + b] = blank

            @pl.when(there)
            def _():
                y_copy(a, b, me_y + b - 1).wait_recv()

        @pl.when(exists(me_x + a - 1, nx))
        def _():
            to_column(a, lambda copy: copy.wait_send())

    for a in (0, 2):
        target = me_x + 1 - a

        @pl.when(exists(target, nx))
        def _():
            x_copy(a, target).wait_send()

    for step in range(1, ny):
        weight_copy(step, lax.rem(me_y - step + ny, ny)).wait_recv()
        weight_copy(step, me_y).wait_send()
    keep.wait()


def compute_kernel(
    source_ref,
    target_ref,
    count_ref,
    feats_ref,
    halo_ref,
    weight_ref,
    bias_ref,
    cot_ref,
    out_ref,
    own_ref,
    borrowed_ref,
    wpart_ref,
    table,
    turned,
    pre,
    dpre,
    grad,
):
    blocks, rows, width = feats_ref.shape
    slots = source_ref.shape[0]
    kvol = weight_ref.shape[0]
    total_blocks = grad.shape[0] - 1
    shared_count = halo_ref.shape[1]
    ny, tiles = wpart_ref.shape[:2]
    share = width // ny
    share_tiles = share // TILE
    places = [(b, feats_ref.at[b]) for b in range(blocks)]
    at = blocks
    for d in range(9):
        if d != 4:
            for s in range(shared_count):
                places.append((at, halo_ref.at[d, s]))
                at += 1
    for t, ref in places:
        value = ref[...]
        table[t] = value
        turned[t] = value.T
    for b in range(blocks):
        pre[b] = jnp.broadcast_to(bias_ref[...], (rows, width))
    for t in range(total_blocks):
        grad[t] = jnp.zeros((rows, width), jnp.float32)
    pre[blocks] = jnp.zeros((rows, width), jnp.float32)
    grad[total_blocks] = jnp.zeros((rows, width), jnp.float32)
    dpre[blocks] = jnp.zeros((rows, width), dpre.dtype)

    def rules(k):
        live = count_ref[k]
        sources = [source_ref[q, k] for q in range(slots)]
        targets = [target_ref[q, k] for q in range(slots)]
        reads = [jnp.where(q < live, v, 0) for q, v in enumerate(sources)]
        spread = [jnp.where(q < live, v, total_blocks) for q, v in enumerate(sources)]
        targets = [jnp.where(q < live, v, blocks) for q, v in enumerate(targets)]
        return reads, spread, targets

    def forward(k, carry):
        reads, _, targets = rules(k)
        taken = jnp.concatenate([table[s] for s in reads], axis=0)
        made = jnp.dot(taken, weight_ref[k], preferred_element_type=jnp.float32)
        for q, target in enumerate(targets):
            pre[target] += made[q * rows : (q + 1) * rows]
        return carry

    lax.fori_loop(0, kvol, forward, 0, unroll=UNROLL)

    def activate(b, carry):
        value = pre[b]
        sig = jax.nn.sigmoid(value)
        out_ref[b] = (value * sig).astype(out_ref.dtype)
        dpre[b] = (cot_ref[b].astype(jnp.float32) * sig * (1.0 + value * (1.0 - sig))).astype(
            dpre.dtype
        )
        return carry

    lax.fori_loop(0, blocks, activate, 0)

    filled = 2 * kvol * share_tiles
    if filled < tiles:
        for y in range(ny):
            wpart_ref[y, filled:] = jnp.zeros((tiles - filled, TILE, LANES), wpart_ref.dtype)

    def backward(k, carry):
        reads, spread, targets = rules(k)
        pulled = jnp.concatenate([dpre[t] for t in targets], axis=0)
        taken = jnp.concatenate([turned[s] for s in reads], axis=1)
        part = jnp.dot(taken, pulled, preferred_element_type=jnp.float32).astype(wpart_ref.dtype)
        for y in range(ny):
            for h in range(width // LANES):
                piece = part[y * share : (y + 1) * share, h * LANES : (h + 1) * LANES]
                wpart_ref[y, pl.ds((h * kvol + k) * share_tiles, share_tiles)] = piece.reshape(
                    share_tiles, TILE, LANES
                )
        back = lax.dot_general(
            pulled, weight_ref[k], (((1,), (1,)), ((), ())), preferred_element_type=jnp.float32
        )
        for q, source in enumerate(spread):
            grad[source] += back[q * rows : (q + 1) * rows]
        return carry

    lax.fori_loop(0, kvol, backward, 0, unroll=UNROLL)
    for b in range(blocks):
        own_ref[b] = grad[b]
    at = blocks
    for d in range(9):
        for s in range(shared_count):
            if d == 4:
                borrowed_ref[d, s] = jnp.zeros((rows, width), borrowed_ref.dtype)
            else:
                borrowed_ref[d, s] = grad[at].astype(borrowed_ref.dtype)
                at += 1


def reduce_kernel(
    nx,
    ny,
    wpart_ref,
    borrowed_ref,
    sum_ref,
    returned_ref,
    work,
    yland,
    xland,
    side_land,
    column,
    x_land,
    ysend,
    yrecv,
    rsend,
    rrecv,
    gsend,
    grecv,
    hsend,
    hrecv,
    bsend,
    brecv,
):
    me_x, me_y = lax.axis_index("gx"), lax.axis_index("gy")
    groups = work.shape[0]
    steps = nx.bit_length() - 1
    bits = [lax.rem(me_x // (1 << b), 2) for b in range(steps)]
    partners = [me_x + (1 - 2 * bits[b]) * (1 << b) for b in range(steps)]

    barrier = pltpu.get_barrier_semaphore()
    expected = greet_neighbours(barrier, me_x, me_y, nx, ny) + greet_column(
        barrier, me_x, me_y, ny
    )
    for b in range(steps):
        pl.semaphore_signal(barrier, inc=1, device_id=(partners[b], me_y), device_id_type=MESH)
    pl.semaphore_wait(barrier, expected + steps)

    def side_copy(a, b):
        return pltpu.make_async_remote_copy(
            src_ref=borrowed_ref.at[3 * a + b],
            dst_ref=side_land.at[a, b // 2],
            send_sem=hsend.at[a, b // 2],
            recv_sem=hrecv.at[a, b // 2],
            device_id=(me_x, me_y + b - 1),
            device_id_type=MESH,
        )

    def back_copy(a):
        return pltpu.make_async_remote_copy(
            src_ref=column.at[a // 2],
            dst_ref=x_land.at[a // 2],
            send_sem=bsend.at[a // 2],
            recv_sem=brecv.at[a // 2],
            device_id=(me_x + a - 1, me_y),
            device_id_type=MESH,
        )

    def sides(act, sign):
        for a in range(3):
            for b in (0, 2):

                @pl.when(exists(me_x + a - 1, nx) & exists(me_y + sign * (b - 1), ny))
                def _():
                    act(a, b)

    def column_copy(step, g):
        other = lax.rem(me_y + step, ny)
        return pltpu.make_async_remote_copy(
            src_ref=wpart_ref.at[other, g],
            dst_ref=yland.at[step - 1, g],
            send_sem=ysend.at[step - 1, g],
            recv_sem=yrecv.at[step - 1, g],
            device_id=(me_x, other),
            device_id_type=MESH,
        )

    late = list(range(2, steps))
    kinds = [[0, 1] + late, [1, 0] + late, late + [0, 1], late + [1, 0]]
    orders = [kinds[kind] for kind in KINDS]
    starts = []
    for g in range(groups):
        at = [0]
        for s in range(steps):
            at.append(at[-1] + bits[orders[g][s]] * (nx >> (s + 1)))
        starts.append(at)

    def scatter_copy(g, s):
        half = nx >> (s + 1)
        bit = bits[orders[g][s]]
        away = starts[g][s] + (1 - bit) * half
        return pltpu.make_async_remote_copy(
            src_ref=work.at[g, pl.ds(away, half)],
            dst_ref=xland.at[g, pl.ds(nx - 2 * half, half)],
            send_sem=rsend.at[s, g],
            recv_sem=rrecv.at[s, g],
            device_id=(partners[orders[g][s]], me_y),
            device_id_type=MESH,
        )

    def gather_copy(g, s, landing):
        half = nx >> (s + 1)
        bit = bits[orders[g][s]]
        mine = starts[g][s + 1]
        place = starts[g][s] + (1 - bit) * half if landing else mine
        return pltpu.make_async_remote_copy(
            src_ref=sum_ref.at[g, pl.ds(mine, half)],
            dst_ref=sum_ref.at[g, pl.ds(place, half)],
            send_sem=gsend.at[s, g],
            recv_sem=grecv.at[s, g],
            device_id=(partners[orders[g][s]], me_y),
            device_id_type=MESH,
        )

    for g in range(groups):
        for step in range(1, ny):
            column_copy(step, g).start()
    sides(lambda a, b: side_copy(a, b).start(), 1)

    def begin(g):
        value = wpart_ref[me_y, g].astype(jnp.float32)
        for step in range(1, ny):
            column_copy(step, g).wait_recv()
            value = value + yland[step - 1, g].astype(jnp.float32)
        work[g] = value.astype(work.dtype)
        scatter_copy(g, 0).start()

    def scatter(g, s):
        half = nx >> (s + 1)
        scatter_copy(g, s).wait_recv()
        keep = pl.ds(starts[g][s + 1], half)
        value = work[g, keep].astype(jnp.float32) + xland[g, pl.ds(nx - 2 * half, half)].astype(
            jnp.float32
        )
        if s < steps - 1:
            work[g, keep] = value.astype(work.dtype)
            scatter_copy(g, s + 1).start()
        else:
            sum_ref[g, keep] = value.astype(sum_ref.dtype)
            gather_copy(g, s, False).start()

    def gather(g, s):
        gather_copy(g, s, True).wait_recv()
        if s > 0:
            gather_copy(g, s - 1, False).start()

    events = []
    for g in range(groups):
        events.append((WAVES[g] * STAGGER, g, functools.partial(begin, g)))
        for s in range(steps):
            events.append((WAVES[g] * STAGGER + s + 1, g, functools.partial(scatter, g, s)))
            events.append(
                (WAVES[g] * STAGGER + 2 * steps - s, g, functools.partial(gather, g, s))
            )
    events.sort(key=lambda event: event[:2])
    first = [event[2] for event in events if event[0] < HALO_AT]
    rest = [event[2] for event in events if event[0] >= HALO_AT]
    for event in first:
        event()

    returned_ref[...] = jnp.zeros(returned_ref.shape, jnp.float32)
    for b in (0, 2):

        @pl.when(exists(me_y + 1 - b, ny))
        def _():
            side_copy(1, b).wait_recv()
            returned_ref[...] += side_land[1, b // 2].astype(jnp.float32)

    for a in (0, 2):

        @pl.when(exists(me_x + a - 1, nx))
        def _():
            for b in (0, 2):
                missing = jnp.logical_not(exists(me_y + 1 - b, ny))

                @pl.when(missing)
                def _():
                    side_land[a, b // 2] = jnp.zeros(side_land.shape[2:], side_land.dtype)

                @pl.when(jnp.logical_not(missing))
                def _():
                    side_copy(a, b).wait_recv()

            column[a // 2] = (
                borrowed_ref[3 * a + 1].astype(jnp.float32)
                + side_land[a, 0].astype(jnp.float32)
                + side_land[a, 1].astype(jnp.float32)
            ).astype(column.dtype)
            back_copy(a).start()

    for event in rest:
        event()

    for a in (0, 2):

        @pl.when(exists(me_x + 1 - a, nx))
        def _():
            back_copy(a).wait_recv()
            returned_ref[...] += x_land[a // 2].astype(jnp.float32)

    for g in range(groups):
        for step in range(1, ny):
            column_copy(step, g).wait_send()
        for s in range(steps):
            scatter_copy(g, s).wait_send()
            gather_copy(g, s, False).wait_send()
    sides(lambda a, b: side_copy(a, b).wait_send(), 1)
    for a in (0, 2):

        @pl.when(exists(me_x + a - 1, nx))
        def _():
            back_copy(a).wait_send()


def finish_kernel(
    send_ref, total_ref, own_ref, returned_ref, weight_ref, feat_ref, wide, feats, wsem, fsem
):
    chunks = wsem.shape[0]
    kvol, share, width = wide.shape
    per = kvol // chunks
    blocks, rows = own_ref.shape[:2]
    copies = []
    for c in range(chunks):
        at = pl.ds(c * per, per)
        for h in range(width // LANES):
            wide[at, :, h * LANES : (h + 1) * LANES] = total_ref[h, at].reshape(
                per, share, LANES
            ).astype(jnp.float32) * (1.0 / rows)
        copy = pltpu.make_async_copy(wide.at[at], weight_ref.at[at], wsem.at[c])
        copy.start()
        copies.append(copy)
    for b in range(blocks):
        value = own_ref[b]
        for s in range(returned_ref.shape[0]):
            value = value + jnp.where(send_ref[s] == b, returned_ref[s], 0.0)
        feats[b] = value.astype(feats.dtype)
        copy = pltpu.make_async_copy(feats.at[b], feat_ref.at[b], fsem.at[b])
        copy.start()
        copies.append(copy)
    for copy in copies:
        copy.wait()


def on_device(
    nx,
    ny,
    features,
    kernel_weight,
    channel_bias,
    send_list,
    rule_source,
    rule_target,
    live_counts,
    out_grad,
):
    feats = features[0, 0]
    blocks, rows, width = feats.shape
    shared = send_list[0, 0]
    shared_count = shared.shape[0]
    kvol, slots = rule_source.shape[2:]
    share = kernel_weight.shape[1]
    bf16, f32 = jnp.bfloat16, jnp.float32
    shape = jax.ShapeDtypeStruct
    vmem = pl.BlockSpec(memory_space=VMEM)
    smem = pl.BlockSpec(memory_space=SMEM)
    hbm = pl.BlockSpec(memory_space=pltpu.HBM)
    dma = pltpu.SemaphoreType.DMA
    squares = 9

    halo, full = pl.pallas_call(
        functools.partial(exchange_kernel, nx, ny),
        out_shape=(
            shape((squares, shared_count, rows, width), bf16),
            shape((kvol, ny, share, width), bf16),
        ),
        in_specs=[smem, hbm, hbm],
        out_specs=(vmem, vmem),
        scratch_shapes=[
            VMEM((blocks, rows, width), bf16),
            dma((2,)),
            dma((2,)),
            dma((2,)),
            dma((3, 2)),
            dma((3, 2)),
            dma((ny,)),
            dma((ny,)),
        ],
        compiler_params=pltpu.CompilerParams(
            collective_id=0, has_side_effects=True, vmem_limit_bytes=EXCHANGE_BYTES
        ),
    )(shared, feats, kernel_weight)

    total_blocks = blocks + (squares - 1) * shared_count
    used = (width // LANES) * kvol * (share // TILE)
    groups = len(KINDS)
    unit = groups * nx
    tiles = -(-used // unit) * unit
    depth = tiles // unit
    outputs, own, borrowed, wpart = pl.pallas_call(
        compute_kernel,
        out_shape=(
            shape((blocks, rows, width), bf16),
            shape((blocks, rows, width), f32),
            shape((squares, shared_count, rows, width), bf16),
            shape((ny, tiles, TILE, LANES), bf16),
        ),
        in_specs=[smem, smem, smem, vmem, vmem, vmem, vmem, vmem],
        out_specs=(vmem, vmem, vmem, vmem),
        scratch_shapes=[
            VMEM((total_blocks, rows, width), bf16),
            VMEM((total_blocks, width, rows), bf16),
            VMEM((blocks + 1, rows, width), f32),
            VMEM((blocks + 1, rows, width), bf16),
            VMEM((total_blocks + 1, rows, width), f32),
        ],
        compiler_params=pltpu.CompilerParams(vmem_limit_bytes=VMEM_BYTES),
    )(
        rule_source[0, 0].T,
        rule_target[0, 0].T,
        live_counts.reshape(-1),
        feats,
        halo,
        full.reshape(kvol, width, width),
        channel_bias.reshape(1, width),
        out_grad[0, 0],
    )

    steps = nx.bit_length() - 1
    block = (depth, TILE, LANES)
    boundary = (shared_count, rows, width)
    total, returned = pl.pallas_call(
        functools.partial(reduce_kernel, nx, ny),
        out_shape=(
            shape((groups, nx) + block, bf16),
            shape(boundary, f32),
        ),
        in_specs=[vmem, vmem],
        out_specs=(vmem, vmem),
        scratch_shapes=[
            VMEM((groups, nx) + block, bf16),
            VMEM((max(ny - 1, 1), groups, nx) + block, bf16),
            VMEM((groups, nx) + block, bf16),
            VMEM((3, 2) + boundary, bf16),
            VMEM((2,) + boundary, bf16),
            VMEM((2,) + boundary, bf16),
            dma((max(ny - 1, 1), groups)),
            dma((max(ny - 1, 1), groups)),
            dma((steps, groups)),
            dma((steps, groups)),
            dma((steps, groups)),
            dma((steps, groups)),
            dma((3, 2)),
            dma((3, 2)),
            dma((2,)),
            dma((2,)),
        ],
        compiler_params=pltpu.CompilerParams(
            collective_id=1, has_side_effects=True, vmem_limit_bytes=VMEM_BYTES
        ),
    )(wpart.reshape((ny, groups, nx) + block), borrowed)

    halves, share_tiles = width // LANES, share // TILE
    chunks = max(c for c in range(1, 10) if kvol % c == 0)
    weight_grad, feat_grad = pl.pallas_call(
        finish_kernel,
        out_shape=(shape((kvol, share, width), f32), shape((blocks, rows, width), bf16)),
        in_specs=[smem, vmem, vmem, vmem],
        out_specs=(hbm, hbm),
        scratch_shapes=[
            VMEM((kvol, share, width), f32),
            VMEM((blocks, rows, width), bf16),
            dma((chunks,)),
            dma((blocks,)),
        ],
        compiler_params=pltpu.CompilerParams(vmem_limit_bytes=VMEM_BYTES),
    )(
        shared,
        total.reshape(tiles, TILE, LANES)[:used].reshape(halves, kvol, share_tiles, TILE, LANES),
        own,
        returned,
    )
    return (outputs[None, None], feat_grad[None, None], weight_grad)


def solution(mesh):
    return jax.shard_map(
        functools.partial(on_device, mesh.shape["gx"], mesh.shape["gy"]),
        mesh=mesh,
        in_specs=(
            P("gx", "gy", None, None, None),
            P(None, "gy", None),
            P(),
            P("gx", "gy", None),
            P("gx", "gy", None, None),
            P("gx", "gy", None, None),
            P("gx", "gy", None),
            P("gx", "gy", None, None, None),
        ),
        out_specs=(
            P("gx", "gy", None, None, None),
            P("gx", "gy", None, None, None),
            P(None, "gy", None),
        ),
        check_vma=False,
    )
```
